32 devices in a mesh: dp: 4 (over x, core), fsdp: 8 (over z, y).
Axes of the slice: x: 2, y: 2, z: 4, core: 2. Of those that a mesh axis runs over, the one named last changes fastest.
Arguments:
- tokens: bfloat16 [8192, 768], P(('dp', 'fsdp')), may hold values from -6 to 6
- cotangent: bfloat16 [8192, 768], P(('dp', 'fsdp')), may hold values from -6 to 6
- starts: int32 [8192], P(('dp', 'fsdp')), may hold values from 0 to 256, as said below
- attention_norm_scale: bfloat16 [768], P(('dp', 'fsdp')), may hold values from 0.5 to 1.5
- w_qkv: bfloat16 [768, 2304], P(('dp', 'fsdp')), may hold values from -3 to 3
- w_out: bfloat16 [768, 768], P(None, ('dp', 'fsdp')), may hold values from -0.875 to 0.875
- feedforward_norm_scale: bfloat16 [768], P(('dp', 'fsdp')), may hold values from 0.5 to 1.5
- w_in: bfloat16 [768, 2304], P(('dp', 'fsdp')), may hold values from -0.21875 to 0.21875
- w_down: bfloat16 [1152, 768], P(None, ('dp', 'fsdp')), may hold values from -0.1875 to 0.1875
Outputs:
- output: bfloat16 [8192, 768], P(('dp', 'fsdp'))
- input_grad: float32 [8192, 768], P(('dp', 'fsdp'))
- w_qkv_grad: float32 [768, 2304], P(('dp', 'fsdp'))
- w_out_grad: float32 [768, 768], P(None, ('dp', 'fsdp'))
- w_in_grad: float32 [768, 2304], P(('dp', 'fsdp'))
- w_down_grad: float32 [1152, 768], P(None, ('dp', 'fsdp'))
- attn_gain_grad: float32 [768], P(('dp', 'fsdp'))
- mlp_gain_grad: float32 [768], P(('dp', 'fsdp'))
The draws below stay inside these ranges and needn't reach their ends.
Inputs may be any that keep to these rules, and one draw needn't show every extreme that they name: `starts`: each sequence lies whole in one block of 256 slots and occupies consecutive slots; a slot's entry is its sequence's first slot within the block. Slots after a block's last sequence are empty and hold 256. In every draw some block has no empty slot and some other block has one or more.
All inputs are finite; a program needn't handle non-finite values.
Results may differ from the reference program's by a relative error of at most 0.012.
Values may be sent and summed in bfloat16 or wider, within the bound.
A program may use at most 128 MiB of HBM per device.

```python
import jax
import jax.numpy as jnp
from jax import lax

D = 768
HEADS = 12
HEAD_DIM = 64
FF = 1152
HALF_WINDOW = 64
TOK_DEV = 256
TOKENS = 8192


def draw_starts(key, part):
    block_count = TOKENS // TOK_DEV
    slot = jnp.arange(TOK_DEV, dtype=jnp.int32)
    spacing = max(TOK_DEV // 2, 2)
    cuts = jax.random.randint(jax.random.fold_in(key, 1), (block_count, TOK_DEV), 0, spacing) == 0
    cuts = cuts | (slot == 0)[None, :]
    first = lax.cummax(jnp.where(cuts, slot[None, :], 0), axis=1)
    padding = jax.random.randint(jax.random.fold_in(key, 2), (block_count,), 0, TOK_DEV // 2 + 1)
    full_block = jax.random.randint(jax.random.fold_in(key, 3), (), 0, block_count)
    short_block = (full_block + 1 + jax.random.randint(jax.random.fold_in(key, 4), (), 0, block_count - 1)) % block_count
    block_index = jnp.arange(block_count, dtype=jnp.int32)
    padding = jnp.where(block_index == full_block, 0, jnp.where(block_index == short_block, jnp.maximum(padding, 1), padding))
    first = jnp.where(slot[None, :] >= TOK_DEV - padding[:, None], TOK_DEV, first)
    return first.reshape(-1).astype(jnp.int32)


def draw_w_qkv(key, part):
    base = jnp.clip(jax.random.normal(key, (D, 3 * D), jnp.float32), -6.0, 6.0)
    scale = D ** (-0.5)
    return (base * scale).astype(jnp.bfloat16)


def strengthened(entries, own_key, source, target, blocks, factor):
    def block_of(dim):
        return (jnp.arange(entries.shape[dim]) // (entries.shape[dim] // blocks)).reshape((-1,) + (1,) * (entries.ndim - 1 - dim))

    near = jax.random.permutation(own_key, blocks)[block_of(target)]
    second = (block_of(target) + blocks // 2) % blocks
    return jnp.where((block_of(source) == near) | (block_of(source) == second), factor * entries, entries)


def steps_of(key, shape, split, smallest, high):
    gain = 1.0
    for axis_at, shards_of in split:
        heights = jax.random.uniform(jax.random.fold_in(jax.random.fold_in(key, 6), axis_at), (shards_of,), jnp.float32, smallest / len(split), high / len(split))
        gain = gain * jnp.repeat(jnp.exp(heights), shape[axis_at] // shards_of).reshape((-1,) + (1,) * (len(shape) - 1 - axis_at))
    return gain


def bell_draw(rng, extent, scale, most, cuts=(), kind=jnp.bfloat16):
    loudness = steps_of(rng, extent, cuts, -0.22, 0.18) if cuts else 1.0
    values = jax.random.normal(rng, extent, jnp.float32) * scale * loudness
    return jnp.minimum(jnp.maximum(values, -most), most).astype(kind)


def gaussian_with(rng, dims, spread, most, split, heavy, kind=jnp.bfloat16):
    array = spread * jax.random.normal(rng, dims, jnp.float32)
    if split:
        array = array * steps_of(rng, dims, split, -0.22, 0.18)
    return jnp.clip(strengthened(array, jax.random.fold_in(rng, 3), *heavy), -most, most).astype(kind)


def setup_inputs(seed: int = 0) -> dict:
    splits = jax.random.split(jax.random.key(seed), 10)
    return {
        "tokens": bell_draw(splits[0], (TOKENS, D), 1.0, 6.0, ((0, 32),)),
        "cotangent": gaussian_with(splits[1], (TOKENS, D), 1.0, 6.0, ((0, 32),), (0, 1, 32, 2.75)),
        "starts": draw_starts(jax.random.fold_in(splits[9], 71), 0),
        "attention_norm_scale": jnp.clip(1.0 + 0.1 * jax.random.normal(splits[3], (D,), jnp.float32), 0.5, 1.5).astype(jnp.bfloat16),
        "w_qkv": draw_w_qkv(jax.random.fold_in(splits[9], 71), 0),
        "w_out": bell_draw(splits[5], (D, D), (D // 16) ** -0.5, 0.875, ((1, 32),)),
        "feedforward_norm_scale": jnp.clip(1.0 + 0.1 * jax.random.normal(splits[6], (D,), jnp.float32), 0.5, 1.5).astype(jnp.bfloat16),
        "w_in": bell_draw(splits[7], (D, 2 * FF), D ** -0.5, 0.21875, ((0, 32),)),
        "w_down": bell_draw(splits[8], (FF, D), FF ** -0.5, 0.1875, ((1, 32),)),
    }


epsilon = 1e-05
rope_base = 10000.0
sqrt_half = 0.7071067811865476
inv_sqrt_tau = 0.3989422804014327
big_negative = -1e+30

def apply_layer_norm(values):
    mean_value = lax.optimization_barrier(jnp.mean(values, axis=-1, keepdims=True))
    centered = values - mean_value
    inverse_deviation = lax.rsqrt(lax.optimization_barrier(jnp.mean(centered * centered, axis=-1, keepdims=True)) + epsilon)
    return (centered * inverse_deviation, inverse_deviation)

def norm_backward(normalized_gradient, standardized_input, inverse_deviation, norm_scale):
    scale_gradient = lax.optimization_barrier(jnp.sum(normalized_gradient * standardized_input, axis=0))
    scaled_output = normalized_gradient * norm_scale
    first_average = lax.optimization_barrier(jnp.mean(scaled_output, axis=-1, keepdims=True))
    second_average = lax.optimization_barrier(jnp.mean(scaled_output * standardized_input, axis=-1, keepdims=True))
    return (inverse_deviation * (scaled_output - first_average - standardized_input * second_average), scale_gradient)

def gelu_parts(pre_act):
    normal_cdf = 0.5 * (1.0 + jax.scipy.special.erf(pre_act * sqrt_half))
    density = jnp.exp(-0.5 * pre_act * pre_act) * inv_sqrt_tau
    return (pre_act * normal_cdf, normal_cdf + pre_act * density)

def rotary_tables(position, head_dim):
    half_dim = head_dim // 2
    exponent = 2.0 * jnp.arange(half_dim).astype(jnp.float32) / head_dim
    frequency = rope_base ** (-exponent)
    angle = position.astype(jnp.float32)[:, None] * frequency[None, :]
    return (jnp.cos(angle)[:, None, :], jnp.sin(angle)[:, None, :])

def rotate(values, cosine, sine):
    half_dim = values.shape[-1] // 2
    first_half = values[..., :half_dim]
    second_half = values[..., half_dim:]
    return jnp.concatenate([first_half * cosine - second_half * sine, second_half * cosine + first_half * sine], -1)

def unrotate(grads, cosine, sine):
    half_dim = grads.shape[-1] // 2
    first_half = grads[..., :half_dim]
    second_half = grads[..., half_dim:]
    return jnp.concatenate([first_half * cosine + second_half * sine, second_half * cosine - first_half * sine], -1)

def mat(left, right):
    return jnp.dot(left, right, preferred_element_type=jnp.float32)

def one_device(block_in, block_cot, block_starts, attention_norm_scale, w_qkv, w_out, feedforward_norm_scale, w_in, w_down):
    row_count = block_in.shape[0]
    width = D
    head_dim = HEAD_DIM
    head_count = HEADS
    units = FF
    scale = head_dim ** (-0.5)
    slot = jnp.arange(row_count, dtype=jnp.int32)
    valid = block_starts < row_count
    position = slot - block_starts
    distance = jnp.abs(slot[:, None] - slot[None, :])
    allowed = (block_starts[:, None] == block_starts[None, :]) & (distance <= HALF_WINDOW)
    input_float = block_in.astype(jnp.float32)
    first_standardized, first_inverse_deviation = apply_layer_norm(input_float)
    first_normalized = (first_standardized * attention_norm_scale.astype(jnp.float32)).astype(jnp.bfloat16)
    projected = mat(first_normalized, w_qkv).reshape(row_count, 3, head_count, head_dim)
    cosine, sine = rotary_tables(position, head_dim)
    queries = rotate(projected[:, 0], cosine, sine).astype(jnp.bfloat16)
    keys_rot = rotate(projected[:, 1], cosine, sine).astype(jnp.bfloat16)
    values_h = projected[:, 2].astype(jnp.bfloat16)
    scores = jnp.einsum('qhd,khd->hqk', queries.astype(jnp.float32), keys_rot.astype(jnp.float32)) * scale
    scores = jnp.where(allowed[None], scores, big_negative)
    top = lax.optimization_barrier(jnp.max(scores, axis=-1, keepdims=True))
    log_total = top + jnp.log(lax.optimization_barrier(jnp.sum(jnp.exp(scores - top), axis=-1, keepdims=True)))
    prob = jnp.exp(scores - log_total)
    prob_b = prob.astype(jnp.bfloat16)
    attended3 = jnp.einsum('hqk,khd->qhd', prob_b.astype(jnp.float32), values_h.astype(jnp.float32)).astype(jnp.bfloat16)
    attended = attended3.reshape(row_count, width)
    hidden_state = input_float + mat(attended, w_out)
    second_standardized, second_inverse_deviation = apply_layer_norm(hidden_state)
    second_normalized = (second_standardized * feedforward_norm_scale.astype(jnp.float32)).astype(jnp.bfloat16)
    gate_up = mat(second_normalized, w_in)
    pre_act = gate_up[:, :units]
    gate_half = gate_up[:, units:]
    activated, slope = gelu_parts(pre_act)
    hidden = (activated * gate_half).astype(jnp.bfloat16)
    output = (hidden_state + mat(hidden, w_down)).astype(jnp.bfloat16)
    grad_out = jnp.where(valid[:, None], block_cot, jnp.zeros_like(block_cot))
    down_grad = mat(hidden.T, grad_out)
    d_hidden = mat(grad_out, w_down.T)
    d_gu = jnp.concatenate([d_hidden * gate_half * slope, d_hidden * activated], 1).astype(jnp.bfloat16)
    in_grad = mat(second_normalized.T, d_gu)
    second_normalized_gradient = mat(d_gu, w_in.T)
    mixed_gradient, feedforward_scale_gradient = norm_backward(second_normalized_gradient, second_standardized, second_inverse_deviation, feedforward_norm_scale.astype(jnp.float32))
    d_state = grad_out.astype(jnp.float32) + mixed_gradient
    d_state_b = d_state.astype(jnp.bfloat16)
    out_grad = mat(attended.T, d_state_b)
    d_attended = mat(d_state_b, w_out.T).astype(jnp.bfloat16).reshape(row_count, head_count, head_dim)
    delta = lax.optimization_barrier(jnp.sum(d_attended.astype(jnp.float32) * attended3.astype(jnp.float32), axis=-1)).T[:, :, None]
    d_prob = jnp.einsum('qhd,khd->hqk', d_attended.astype(jnp.float32), values_h.astype(jnp.float32))
    d_scores = (prob * (d_prob - delta) * scale).astype(jnp.bfloat16)
    d_value = jnp.einsum('hqk,qhd->khd', prob_b.astype(jnp.float32), d_attended.astype(jnp.float32))
    d_query = jnp.einsum('hqk,khd->qhd', d_scores.astype(jnp.float32), keys_rot.astype(jnp.float32))
    d_key = jnp.einsum('hqk,qhd->khd', d_scores.astype(jnp.float32), queries.astype(jnp.float32))
    d_qkv = jnp.stack([unrotate(d_query, cosine, sine), unrotate(d_key, cosine, sine), d_value], 1)
    d_qkv = d_qkv.reshape(row_count, 3 * width).astype(jnp.bfloat16)
    qkv_grad = mat(first_normalized.T, d_qkv)
    first_normalized_gradient = mat(d_qkv, w_qkv.T)
    norm_input_gradient, attention_scale_gradient = norm_backward(first_normalized_gradient, first_standardized, first_inverse_deviation, attention_norm_scale.astype(jnp.float32))
    input_grad = d_state + norm_input_gradient
    return (output, input_grad, (qkv_grad, out_grad, in_grad, down_grad, attention_scale_gradient, feedforward_scale_gradient))

def reference(tokens, cotangent, starts, attention_norm_scale, w_qkv, w_out, feedforward_norm_scale, w_in, w_down):
    block_count = TOKENS // TOK_DEV
    tok_blocks = tokens.reshape(block_count, TOK_DEV, D)
    cot_blocks = cotangent.reshape(block_count, TOK_DEV, D)
    start_blocks = starts.reshape(block_count, TOK_DEV)
    zeros_init = (jnp.zeros((D, 3 * D), jnp.float32), jnp.zeros((D, D), jnp.float32), jnp.zeros((D, 2 * FF), jnp.float32), jnp.zeros((FF, D), jnp.float32), jnp.zeros((D,), jnp.float32), jnp.zeros((D,), jnp.float32))

    def step_block(totals, operands):
        block_in, block_cot, block_starts = operands
        output, input_grad, grads = one_device(block_in, block_cot, block_starts, attention_norm_scale, w_qkv, w_out, feedforward_norm_scale, w_in, w_down)
        totals = tuple((total + grad for total, grad in zip(totals, grads)))
        return (totals, (output, input_grad))
    totals, (outputs, input_grads) = lax.scan(step_block, zeros_init, (tok_blocks, cot_blocks, start_blocks))
    return (outputs.reshape(TOKENS, D), input_grads.reshape(TOKENS, D), totals[0], totals[1], totals[2], totals[3], totals[4], totals[5])
```

```python
import functools

import jax
import jax.numpy as jnp
from jax import lax
from jax.experimental import pallas as pl
from jax.experimental.pallas import tpu as pltpu
from jax.sharding import PartitionSpec as P

HEAD_DIM = 64
HALF_WINDOW = 64


epsilon = 1e-05
rope_base = 10000.0
sqrt_half = 0.7071067811865476
inv_sqrt_tau = 0.3989422804014327
big_negative = -1e30


def apply_layer_norm(values):
    mean_value = jnp.mean(values, axis=-1, keepdims=True)
    centered = values - mean_value
    inverse_deviation = lax.rsqrt(jnp.mean(centered * centered, axis=-1, keepdims=True) + epsilon)
    return (centered * inverse_deviation, inverse_deviation)


def norm_backward(normalized_gradient, standardized_input, inverse_deviation, norm_scale):
    scale_gradient = jnp.sum(normalized_gradient * standardized_input, axis=0)
    scaled_output = normalized_gradient * norm_scale
    first_average = jnp.mean(scaled_output, axis=-1, keepdims=True)
    second_average = jnp.mean(scaled_output * standardized_input, axis=-1, keepdims=True)
    return (
        inverse_deviation * (scaled_output - first_average - standardized_input * second_average),
        scale_gradient,
    )


def gelu_parts(pre_act):
    normal_cdf = 0.5 * (1.0 + jax.scipy.special.erf(pre_act * sqrt_half))
    density = jnp.exp(-0.5 * pre_act * pre_act) * inv_sqrt_tau
    return (pre_act * normal_cdf, normal_cdf + pre_act * density)


def rotary_tables(position, head_dim):
    half_dim = head_dim // 2
    exponent = 2.0 * jnp.arange(half_dim).astype(jnp.float32) / head_dim
    frequency = rope_base ** (-exponent)
    angle = position.astype(jnp.float32)[:, None] * frequency[None, :]
    return (jnp.cos(angle), jnp.sin(angle))


def rotate(values, cosine, sine):
    half_dim = values.shape[-1] // 2
    first_half = values[..., :half_dim]
    second_half = values[..., half_dim:]
    return jnp.concatenate(
        [first_half * cosine - second_half * sine, second_half * cosine + first_half * sine], -1
    )


def unrotate(grads, cosine, sine):
    half_dim = grads.shape[-1] // 2
    first_half = grads[..., :half_dim]
    second_half = grads[..., half_dim:]
    return jnp.concatenate(
        [first_half * cosine + second_half * sine, second_half * cosine - first_half * sine], -1
    )


def contract_rows(left, right):
    return lax.dot_general(
        left, right, (((0,), (0,)), ((), ())), preferred_element_type=jnp.float32
    )


def times_transposed(left, right):
    return lax.dot_general(
        left, right, (((1,), (1,)), ((), ())), preferred_element_type=jnp.float32
    )


MESH = pl.DeviceIdType.MESH
LANES = 128


def split_pair(count):
    inner = 2 if count % 2 == 0 else 1
    return count // inner, inner


class Grid:
    def __init__(self, dp, fsdp):
        x, c = split_pair(dp)
        z, y = split_pair(fsdp)
        self.size = {"x": x, "c": c, "z": z, "y": y}

    def here(self):
        d, f = lax.axis_index("dp"), lax.axis_index("fsdp")
        c, y = self.size["c"], self.size["y"]
        return {"x": lax.div(d, c), "c": lax.rem(d, c), "z": lax.div(f, y), "y": lax.rem(f, y)}

    def step(self, at, axis, k):
        return {**at, axis: lax.rem(at[axis] + k, self.size[axis])}

    def device(self, at):
        return (at["x"] * self.size["c"] + at["c"], at["z"] * self.size["y"] + at["y"])

    def shape(self):
        return tuple(self.size[a] for a in "xczy")

    def barrier(self, at):
        sem = pltpu.get_barrier_semaphore()
        total = 0
        for axis in "xczy":
            for k in range(1, self.size[axis]):
                pl.semaphore_signal(
                    sem, inc=1, device_id=self.device(self.step(at, axis, k)), device_id_type=MESH
                )
                total += 1
        pl.semaphore_wait(sem, total)


def schedule(chunks, stages, skew):
    events = [(ci + skew * s, ci, s) for ci in range(chunks) for s in range(stages)]
    return [(ci, s) for _, ci, s in sorted(events)]


def gather_kernel(grid, chunks, count, *refs):
    ins, outs = refs[:count], refs[count : 2 * count]
    local_sem, send_sem, recv_sem = refs[2 * count :]
    at = grid.here()
    grid.barrier(at)
    locals_ = []
    for i in range(count):
        index = tuple(pl.ds(at[a], 1) for a in "xczy")
        copy = pltpu.make_async_copy(ins[i], outs[i].at[index], local_sem.at[i])
        copy.start()
        locals_.append(copy)
    waited = set()
    number = 0
    flying = {}
    for ci, s in schedule(len(chunks), 5, 1.5):
        array, low, width, order = chunks[ci]
        columns = pl.ds(low, width)
        if s > 0:
            if array not in waited:
                locals_[array].wait()
                waited.add(array)
            for copy in flying[ci, s - 1]:
                copy.wait_recv()
        if s == 4:
            continue
        done = order[:s]
        index = tuple(pl.ds(0, grid.size[a]) if a in done else pl.ds(at[a], 1) for a in "xczy")
        block = outs[array].at[index + (slice(None), columns)]
        source = ins[array].at[:, :, :, :, :, columns] if s == 0 else block
        flying[ci, s] = []
        for k in range(1, grid.size[order[s]]):
            copy = pltpu.make_async_remote_copy(
                src_ref=source,
                dst_ref=block,
                send_sem=send_sem.at[number],
                recv_sem=recv_sem.at[number],
                device_id=grid.device(grid.step(at, order[s], k)),
                device_id_type=MESH,
            )
            copy.start()
            number += 1
            flying[ci, s].append(copy)
    for copies in flying.values():
        for copy in copies:
            copy.wait_send()


def gather_all(grid, arrays, chunks):
    per_chunk = sum(n - 1 for n in grid.size.values())
    copies = per_chunk * len(chunks)
    shaped = [a.reshape((1, 1, 1, 1) + a.shape) for a in arrays]
    return pl.pallas_call(
        functools.partial(gather_kernel, grid, chunks, len(arrays)),
        out_shape=[jax.ShapeDtypeStruct(grid.shape() + a.shape, a.dtype) for a in arrays],
        in_specs=[pl.BlockSpec(memory_space=pl.ANY)] * len(arrays),
        out_specs=[pl.BlockSpec(memory_space=pl.ANY)] * len(arrays),
        scratch_shapes=[
            pltpu.SemaphoreType.DMA((len(arrays),)),
            pltpu.SemaphoreType.DMA((copies,)),
            pltpu.SemaphoreType.DMA((copies,)),
        ],
        compiler_params=pltpu.CompilerParams(collective_id=0, has_side_effects=True),
        name="gather_weights",
    )(*shaped)


def scatter_kernel(grid, chunks, count, *refs):
    ins, outs = refs[:count], refs[count : 2 * count]
    rest = refs[2 * count :]
    held = rest[: len(chunks)]
    landed = rest[len(chunks) : 5 * len(chunks)]
    local_sem, send_sem, recv_sem = rest[5 * len(chunks) :]
    at = grid.here()
    grid.barrier(at)
    number = 0
    flying, locals_ = {}, []
    for ci, s in schedule(len(chunks), 5, 1.5):
        array, low, width, order = chunks[ci]
        columns = pl.ds(low, width)
        if s > 0:
            if s == 1:
                locals_[ci].wait()
            for copy in flying[ci, s - 1]:
                copy.wait_recv()
            done = order[:s]
            arrived = landed[4 * ci + s - 1]
            sizes = [1 if a in done else grid.size[a] for a in "xczy"]
            fixed = [
                0 if a == "c" else (at[a] if a in done else None) for a in "xczy"
            ]
            total = sizes[0] * sizes[1] * sizes[2] * sizes[3]
            peers = grid.size[order[s - 1]] - 1

            def add(i, carry, s=s, ci=ci, array=array, columns=columns, sizes=sizes, fixed=fixed,
                    arrived=arrived, peers=peers):
                place, spot, left = [], [], i
                for n, at_fixed in reversed(list(zip(sizes, fixed))):
                    part = 0 if n == 1 else lax.rem(left, n)
                    left = left if n == 1 else lax.div(left, n)
                    spot.append(part)
                    place.append(part if at_fixed is None else at_fixed)
                place, spot = tuple(reversed(place)), tuple(reversed(spot))
                value = held[ci][place].astype(jnp.float32)
                for k in range(peers):
                    value = value + arrived[(k,) + spot].astype(jnp.float32)
                if s == 4:
                    outs[array][:, columns] = value
                else:
                    held[ci][place] = value.astype(held[ci].dtype)
                return carry

            if total == 1:
                add(0, 0)
            else:
                lax.fori_loop(0, total, add, 0)
        if s == 4:
            continue
        axis = order[s]
        done = order[:s]
        if s == 0:
            index = tuple(pl.ds(at[a], 1) if a == "c" else slice(None) for a in "xczy")
            copy = pltpu.make_async_copy(
                ins[array].at[index + (slice(None), columns)], held[ci], local_sem.at[ci]
            )
            copy.start()
            locals_.append(copy)
        flying[ci, s] = []
        for k in range(1, grid.size[axis]):
            target = grid.step(at, axis, k)
            index = []
            for a in "xczy":
                if a == axis:
                    index.append(pl.ds(target[a], 1))
                elif a in done and a != "c":
                    index.append(pl.ds(at[a], 1))
                else:
                    index.append(slice(None))
            index = tuple(index)
            if s == 0:
                source = ins[array].at[index + (slice(None), columns)]
            else:
                source = held[ci].at[index]
            copy = pltpu.make_async_remote_copy(
                src_ref=source,
                dst_ref=landed[4 * ci + s].at[k - 1],
                send_sem=send_sem.at[number],
                recv_sem=recv_sem.at[number],
                device_id=grid.device(target),
                device_id_type=MESH,
            )
            copy.start()
            number += 1
            flying[ci, s].append(copy)
    for copies in flying.values():
        for copy in copies:
            copy.wait_send()


def scatter_sums(grid, arrays, chunks):
    per_chunk = sum(n - 1 for n in grid.size.values())
    copies = per_chunk * len(chunks)
    held, landed = [], []
    for array, _, width, order in chunks:
        dtype, rows = arrays[array].dtype, arrays[array].shape[-2]
        shape = [1 if a == "c" else grid.size[a] for a in "xczy"] + [rows, width]
        held.append(pltpu.VMEM(tuple(shape), dtype))
        for s in range(4):
            part = [1 if a in order[: s + 1] else grid.size[a] for a in "xczy"] + [rows, width]
            landed.append(pltpu.VMEM((max(grid.size[order[s]] - 1, 1),) + tuple(part), dtype))
    return pl.pallas_call(
        functools.partial(scatter_kernel, grid, chunks, len(arrays)),
        out_shape=[jax.ShapeDtypeStruct(a.shape[-2:], jnp.float32) for a in arrays],
        in_specs=[pl.BlockSpec(memory_space=pl.ANY)] * len(arrays),
        out_specs=[pl.BlockSpec(memory_space=pltpu.VMEM)] * len(arrays),
        scratch_shapes=held
        + landed
        + [
            pltpu.SemaphoreType.DMA((len(chunks),)),
            pltpu.SemaphoreType.DMA((copies,)),
            pltpu.SemaphoreType.DMA((copies,)),
        ],
        compiler_params=pltpu.CompilerParams(
            collective_id=1, has_side_effects=True, vmem_limit_bytes=48 * 1024 * 1024
        ),
        name="scatter_grads",
    )(*arrays)


def swap_halves(values, first_half, half_dim):
    lanes = values.shape[-1]
    down = pltpu.roll(values, lanes - half_dim, 1)
    up = pltpu.roll(values, half_dim, 1)
    return jnp.where(first_half, down, up)


def lane_masks(rows):
    lane = lax.broadcasted_iota(jnp.int32, (rows, LANES), 1)
    return lane, lax.rem(lane, HEAD_DIM) < HEAD_DIM // 2


def forward_kernel(scale, q_ref, k_ref, v_ref, cos_ref, sin_ref, col_ref, row_ref,
                   rq_ref, rk_ref, rv_ref, att_ref, prob_ref):
    rows = q_ref.shape[0]
    lane, first_half = lane_masks(rows)
    cosine, sine = cos_ref[...], sin_ref[...]
    q, k = q_ref[...], k_ref[...]
    half = HEAD_DIM // 2
    rq = (q * cosine + swap_halves(q, first_half, half) * sine).astype(jnp.bfloat16)
    rk = (k * cosine + swap_halves(k, first_half, half) * sine).astype(jnp.bfloat16)
    rv = v_ref[...].astype(jnp.bfloat16)
    rq_ref[...], rk_ref[...], rv_ref[...] = rq, rk, rv
    i = lax.broadcasted_iota(jnp.int32, (rows, rows), 0)
    j = lax.broadcasted_iota(jnp.int32, (rows, rows), 1)
    allowed = (col_ref[...] == row_ref[...]) & (jnp.abs(i - j) <= HALF_WINDOW)
    result = jnp.zeros((rows, LANES), jnp.float32)
    for h in range(LANES // HEAD_DIM):
        mine = lax.div(lane, HEAD_DIM) == h
        scores = times_transposed(jnp.where(mine, rq, jnp.zeros_like(rq)), rk) * scale
        scores = jnp.where(allowed, scores, big_negative)
        top = jnp.max(scores, axis=-1, keepdims=True)
        weights = jnp.exp(scores - top)
        prob = weights * (1.0 / jnp.sum(weights, axis=-1, keepdims=True))
        prob_ref[h] = prob
        part = jnp.dot(prob.astype(jnp.bfloat16), rv, preferred_element_type=jnp.float32)
        result = jnp.where(mine, part, result)
    att_ref[...] = result.astype(jnp.bfloat16)


def backward_kernel(scale, rq_ref, rk_ref, rv_ref, att_ref, datt_ref, prob_ref, cos_ref, sin_ref,
                    out_ref):
    rows = rq_ref.shape[0]
    width = out_ref.shape[1] // 3
    lane, first_half = lane_masks(rows)
    rq, rk, rv, datt = rq_ref[...], rk_ref[...], rv_ref[...], datt_ref[...]
    product = datt.astype(jnp.float32) * att_ref[...].astype(jnp.float32)
    dq = jnp.zeros((rows, LANES), jnp.float32)
    dk, dv = dq, dq
    for h in range(LANES // HEAD_DIM):
        mine = lax.div(lane, HEAD_DIM) == h
        delta = jnp.sum(jnp.where(mine, product, 0.0), axis=-1, keepdims=True)
        dprob = times_transposed(jnp.where(mine, datt, jnp.zeros_like(datt)), rv)
        prob = prob_ref[h]
        dscores = (prob * (dprob - delta) * scale).astype(jnp.bfloat16)
        dv = jnp.where(mine, contract_rows(prob.astype(jnp.bfloat16), datt), dv)
        dq = jnp.where(mine, jnp.dot(dscores, rk, preferred_element_type=jnp.float32), dq)
        dk = jnp.where(mine, contract_rows(dscores, rq), dk)
    cosine, sine = cos_ref[...], sin_ref[...]
    half = HEAD_DIM // 2
    dq = dq * cosine - swap_halves(dq, first_half, half) * sine
    dk = dk * cosine - swap_halves(dk, first_half, half) * sine
    at = pl.program_id(0) * LANES
    for part, value in enumerate((dq, dk, dv)):
        columns = pl.ds(pl.multiple_of(part * width + at, LANES), LANES)
        out_ref[:, columns] = value.astype(jnp.bfloat16)


def attention_forward(projected, cosine, sine, starts, scale):
    rows, width = projected.shape[0], projected.shape[1] // 3
    pairs = width // LANES
    heads = LANES // HEAD_DIM
    block = lambda offset: pl.BlockSpec((rows, LANES), lambda j: (0, j + offset))
    whole = lambda shape: pl.BlockSpec(shape, lambda j: (0, 0))
    wide = jax.ShapeDtypeStruct((rows, width), jnp.bfloat16)
    return pl.pallas_call(
        functools.partial(forward_kernel, scale),
        grid=(pairs,),
        in_specs=[block(0), block(pairs), block(2 * pairs), whole((rows, LANES)),
                  whole((rows, LANES)), whole((rows, 1)), whole((1, rows))],
        out_specs=[block(0)] * 4 + [pl.BlockSpec((heads, rows, rows), lambda j: (j, 0, 0))],
        out_shape=[wide] * 4 + [jax.ShapeDtypeStruct((pairs * heads, rows, rows), jnp.float32)],
        name="attention_forward",
    )(projected, projected, projected, cosine, sine, starts[:, None], starts[None, :])


def attention_backward(rq, rk, rv, attended, d_attended, prob, cosine, sine, scale):
    rows, width = rq.shape
    pairs = width // LANES
    heads = LANES // HEAD_DIM
    block = pl.BlockSpec((rows, LANES), lambda j: (0, j))
    whole = lambda shape: pl.BlockSpec(shape, lambda j: (0, 0))
    return pl.pallas_call(
        functools.partial(backward_kernel, scale),
        grid=(pairs,),
        in_specs=[block] * 5 + [pl.BlockSpec((heads, rows, rows), lambda j: (j, 0, 0)),
                  whole((rows, LANES)), whole((rows, LANES))],
        out_specs=whole((rows, 3 * width)),
        out_shape=jax.ShapeDtypeStruct((rows, 3 * width), jnp.bfloat16),
        name="attention_backward",
    )(rq, rk, rv, attended, d_attended, prob, cosine, sine)


def halves(array, columns, first, second):
    if columns % (2 * LANES):
        return [(array, 0, columns, first)]
    half = columns // 2
    return [(array, 0, half, first), (array, half, half, second)]


def body(
    grid,
    tokens,
    cotangent,
    starts,
    attention_norm_scale,
    w_qkv,
    w_out,
    feedforward_norm_scale,
    w_in,
    w_down,
):
    row_count, width = tokens.shape
    units = w_down.shape[0]
    scale = HEAD_DIM ** (-0.5)
    owned = w_qkv.shape[0]
    devices = width // owned
    axes = ("dp", "fsdp")
    kernels = owned % 8 == 0 and owned <= LANES
    out_t, down_t = w_out.T, w_down.T
    if kernels:
        scales = jnp.pad(
            jnp.stack([attention_norm_scale, feedforward_norm_scale]),
            ((0, 14), (0, LANES - owned)),
        )
        parts = [scales, w_qkv, out_t, w_in, down_t]
        zyx, zxy = ("z", "y", "x", "c"), ("z", "x", "y", "c")
        chunks = [(0, 0, LANES, zyx)]
        chunks += halves(1, w_qkv.shape[1], zyx, zxy)
        chunks += halves(2, width, zyx, zxy)
        chunks += halves(3, w_in.shape[1], zyx, zxy)
        chunks += halves(4, units, zxy, zyx)
        all_scales, full_qkv, full_out_t, full_in, full_down_t = gather_all(grid, parts, chunks)
        all_scales = all_scales.reshape(devices, 16, LANES)
        attention_scale = all_scales[:, 0, :owned].reshape(width)
        feedforward_scale = all_scales[:, 1, :owned].reshape(width)
        full_qkv, full_out_t, full_in, full_down_t = (
            a.reshape(width, a.shape[-1]) for a in (full_qkv, full_out_t, full_in, full_down_t)
        )
    else:
        full_qkv, full_out_t, full_in, full_down_t, attention_scale, feedforward_scale = (
            lax.all_gather(a, axes, axis=0, tiled=True)
            for a in (w_qkv, out_t, w_in, down_t, attention_norm_scale, feedforward_norm_scale)
        )
    attention_scale = attention_scale.astype(jnp.float32)
    feedforward_scale = feedforward_scale.astype(jnp.float32)
    slot = jnp.arange(row_count, dtype=jnp.int32)
    valid = starts < row_count
    position = slot - starts
    input_float = tokens.astype(jnp.float32)
    first_standardized, first_inverse_deviation = apply_layer_norm(input_float)
    first_normalized = (first_standardized * attention_scale).astype(jnp.bfloat16)
    projected = jnp.dot(first_normalized, full_qkv, preferred_element_type=jnp.float32)
    cosine, sine = rotary_tables(position, HEAD_DIM)
    repeats = LANES // HEAD_DIM
    cosine = jnp.tile(jnp.concatenate([cosine, cosine], 1), (1, repeats))
    sine = jnp.tile(jnp.concatenate([-sine, sine], 1), (1, repeats))
    rq, rk, rv, attended, prob = attention_forward(projected, cosine, sine, starts, scale)
    hidden_state = input_float + times_transposed(attended, full_out_t)
    second_standardized, second_inverse_deviation = apply_layer_norm(hidden_state)
    second_normalized = (second_standardized * feedforward_scale).astype(jnp.bfloat16)
    gate_up = jnp.dot(second_normalized, full_in, preferred_element_type=jnp.float32)
    pre_act = gate_up[:, :units]
    gate_half = gate_up[:, units:]
    activated, slope = gelu_parts(pre_act)
    hidden = (activated * gate_half).astype(jnp.bfloat16)
    output = (hidden_state + times_transposed(hidden, full_down_t)).astype(jnp.bfloat16)
    grad_out = jnp.where(valid[:, None], cotangent, jnp.zeros_like(cotangent))
    down_grad_t = contract_rows(grad_out, hidden)
    d_hidden = jnp.dot(grad_out, full_down_t, preferred_element_type=jnp.float32)
    d_gu = jnp.concatenate([d_hidden * gate_half * slope, d_hidden * activated], 1).astype(
        jnp.bfloat16
    )
    second_normalized_gradient = times_transposed(d_gu, full_in)
    mixed_gradient, feedforward_scale_gradient = norm_backward(
        second_normalized_gradient,
        second_standardized,
        second_inverse_deviation,
        feedforward_scale,
    )
    d_state = grad_out.astype(jnp.float32) + mixed_gradient
    d_state_b = d_state.astype(jnp.bfloat16)
    out_grad_t = contract_rows(d_state_b, attended)
    d_attended = jnp.dot(d_state_b, full_out_t, preferred_element_type=jnp.float32).astype(
        jnp.bfloat16
    )
    d_qkv = attention_backward(rq, rk, rv, attended, d_attended, prob, cosine, sine, scale)
    first_normalized_gradient = times_transposed(d_qkv, full_qkv)
    norm_input_gradient, attention_scale_gradient = norm_backward(
        first_normalized_gradient,
        first_standardized,
        first_inverse_deviation,
        attention_scale,
    )
    input_grad = d_state + norm_input_gradient
    qkv_whole = contract_rows(first_normalized, d_qkv)
    in_whole = contract_rows(second_normalized, d_gu)
    every_grad = (in_whole, down_grad_t, out_grad_t, qkv_whole)
    gains = (attention_scale_gradient, feedforward_scale_gradient)
    if kernels:
        gains = jnp.stack(gains).reshape(2, devices, owned).transpose(1, 0, 2)
        gains = jnp.pad(gains, ((0, 0), (0, 6), (0, LANES - owned)))
        parts = [a.astype(jnp.bfloat16).reshape(grid.shape() + (owned, a.shape[-1])) for a in every_grad]
        parts.append(gains.reshape(grid.shape() + (8, LANES)))
        xyz, yxz = ("c", "x", "y", "z"), ("c", "y", "x", "z")
        chunks = halves(0, in_whole.shape[1], xyz, yxz)
        chunks += halves(1, units, xyz, yxz)
        chunks += halves(2, width, yxz, xyz)
        chunks += halves(3, qkv_whole.shape[1], xyz, yxz)
        chunks += [(4, 0, LANES, xyz)]
        in_owned, down_owned_t, out_owned_t, qkv_owned, gains = scatter_sums(grid, parts, chunks)
        gain_a_owned, gain_m_owned = gains[0, :owned], gains[1, :owned]
    else:
        in_owned, down_owned_t, out_owned_t, qkv_owned, gain_a_owned, gain_m_owned = (
            lax.psum_scatter(a, axes, scatter_dimension=0, tiled=True) for a in every_grad + gains
        )
    return (
        output,
        input_grad,
        qkv_owned,
        out_owned_t.T,
        in_owned,
        down_owned_t.T,
        gain_a_owned,
        gain_m_owned,
    )


def solution(mesh):
    return jax.shard_map(
        functools.partial(body, Grid(mesh.shape["dp"], mesh.shape["fsdp"])),
        mesh=mesh,
        in_specs=(
            P(("dp", "fsdp"), None),
            P(("dp", "fsdp"), None),
            P(("dp", "fsdp")),
            P(("dp", "fsdp")),
            P(("dp", "fsdp"), None),
            P(None, ("dp", "fsdp")),
            P(("dp", "fsdp")),
            P(("dp", "fsdp"), None),
            P(None, ("dp", "fsdp")),
        ),
        out_specs=(
            P(("dp", "fsdp"), None),
            P(("dp", "fsdp"), None),
            P(("dp", "fsdp"), None),
            P(None, ("dp", "fsdp")),
            P(("dp", "fsdp"), None),
            P(None, ("dp", "fsdp")),
            P(("dp", "fsdp")),
            P(("dp", "fsdp")),
        ),
        check_vma=False,
    )
```

```python
import functools

import jax
import jax.numpy as jnp
from jax import lax
from jax.experimental import pallas as pl
from jax.experimental.pallas import tpu as pltpu
from jax.sharding import PartitionSpec as P

HEAD_DIM = 64
HALF_WINDOW = 64


epsilon = 1e-05
rope_base = 10000.0
sqrt_half = 0.7071067811865476
inv_sqrt_tau = 0.3989422804014327
big_negative = -1e30


def apply_layer_norm(values):
    mean_value = jnp.mean(values, axis=-1, keepdims=True)
    centered = values - mean_value
    inverse_deviation = lax.rsqrt(jnp.mean(centered * centered, axis=-1, keepdims=True) + epsilon)
    return (centered * inverse_deviation, inverse_deviation)


def norm_backward(normalized_gradient, standardized_input, inverse_deviation, norm_scale):
    scale_gradient = jnp.sum(normalized_gradient * standardized_input, axis=0)
    scaled_output = normalized_gradient * norm_scale
    first_average = jnp.mean(scaled_output, axis=-1, keepdims=True)
    second_average = jnp.mean(scaled_output * standardized_input, axis=-1, keepdims=True)
    return (
        inverse_deviation * (scaled_output - first_average - standardized_input * second_average),
        scale_gradient,
    )


def gelu_parts(pre_act):
    normal_cdf = 0.5 * (1.0 + jax.scipy.special.erf(pre_act * sqrt_half))
    density = jnp.exp(-0.5 * pre_act * pre_act) * inv_sqrt_tau
    return (pre_act * normal_cdf, normal_cdf + pre_act * density)


def rotary_tables(position, head_dim):
    half_dim = head_dim // 2
    exponent = 2.0 * jnp.arange(half_dim).astype(jnp.float32) / head_dim
    frequency = rope_base ** (-exponent)
    angle = position.astype(jnp.float32)[:, None] * frequency[None, :]
    return (jnp.cos(angle), jnp.sin(angle))


def rotate(values, cosine, sine):
    half_dim = values.shape[-1] // 2
    first_half = values[..., :half_dim]
    second_half = values[..., half_dim:]
    return jnp.concatenate(
        [first_half * cosine - second_half * sine, second_half * cosine + first_half * sine], -1
    )


def unrotate(grads, cosine, sine):
    half_dim = grads.shape[-1] // 2
    first_half = grads[..., :half_dim]
    second_half = grads[..., half_dim:]
    return jnp.concatenate(
        [first_half * cosine + second_half * sine, second_half * cosine - first_half * sine], -1
    )


def contract_rows(left, right):
    return lax.dot_general(
        left, right, (((0,), (0,)), ((), ())), preferred_element_type=jnp.float32
    )


def times_transposed(left, right):
    return lax.dot_general(
        left, right, (((1,), (1,)), ((), ())), preferred_element_type=jnp.float32
    )


MESH = pl.DeviceIdType.MESH
LANES = 128


def split_pair(count):
    inner = 2 if count % 2 == 0 else 1
    return count // inner, inner


class Grid:
    def __init__(self, dp, fsdp):
        x, c = split_pair(dp)
        z, y = split_pair(fsdp)
        self.size = {"x": x, "c": c, "z": z, "y": y}

    def here(self):
        d, f = lax.axis_index("dp"), lax.axis_index("fsdp")
        c, y = self.size["c"], self.size["y"]
        return {"x": lax.div(d, c), "c": lax.rem(d, c), "z": lax.div(f, y), "y": lax.rem(f, y)}

    def step(self, at, axis, k):
        return {**at, axis: lax.rem(at[axis] + k, self.size[axis])}

    def device(self, at):
        return (at["x"] * self.size["c"] + at["c"], at["z"] * self.size["y"] + at["y"])

    def shape(self):
        return tuple(self.size[a] for a in "xczy")

    def barrier(self, at):
        sem = pltpu.get_barrier_semaphore()
        total = 0
        for axis in "xczy":
            for k in range(1, self.size[axis]):
                pl.semaphore_signal(
                    sem, inc=1, device_id=self.device(self.step(at, axis, k)), device_id_type=MESH
                )
                total += 1
        pl.semaphore_wait(sem, total)


def schedule(chunks, stages, skew):
    events = [(ci + skew * s, ci, s) for ci in range(chunks) for s in range(stages)]
    return [(ci, s) for _, ci, s in sorted(events)]


def gather_kernel(grid, chunks, count, *refs):
    ins, outs = refs[:count], refs[count : 2 * count]
    local_sem, send_sem, recv_sem = refs[2 * count :]
    at = grid.here()
    grid.barrier(at)
    locals_ = []
    for i in range(count):
        index = tuple(pl.ds(at[a], 1) for a in "xczy")
        copy = pltpu.make_async_copy(ins[i], outs[i].at[index], local_sem.at[i])
        copy.start()
        locals_.append(copy)
    waited = set()
    number = 0
    flying = {}
    for ci, s in schedule(len(chunks), 5, 6):
        array, low, width, order = chunks[ci]
        columns = pl.ds(low, width)
        if s > 0:
            if array not in waited:
                locals_[array].wait()
                waited.add(array)
            for copy in flying[ci, s - 1]:
                copy.wait_recv()
        if s == 4:
            continue
        done = order[:s]
        index = tuple(pl.ds(0, grid.size[a]) if a in done else pl.ds(at[a], 1) for a in "xczy")
        block = outs[array].at[index + (slice(None), columns)]
        source = ins[array].at[:, :, :, :, :, columns] if s == 0 else block
        flying[ci, s] = []
        for k in range(1, grid.size[order[s]]):
            copy = pltpu.make_async_remote_copy(
                src_ref=source,
                dst_ref=block,
                send_sem=send_sem.at[number],
                recv_sem=recv_sem.at[number],
                device_id=grid.device(grid.step(at, order[s], k)),
                device_id_type=MESH,
            )
            copy.start()
            number += 1
            flying[ci, s].append(copy)
    for copies in flying.values():
        for copy in copies:
            copy.wait_send()


def gather_all(grid, arrays, chunks):
    per_chunk = sum(n - 1 for n in grid.size.values())
    copies = per_chunk * len(chunks)
    shaped = [a.reshape((1, 1, 1, 1) + a.shape) for a in arrays]
    return pl.pallas_call(
        functools.partial(gather_kernel, grid, chunks, len(arrays)),
        out_shape=[jax.ShapeDtypeStruct(grid.shape() + a.shape, a.dtype) for a in arrays],
        in_specs=[pl.BlockSpec(memory_space=pl.ANY)] * len(arrays),
        out_specs=[pl.BlockSpec(memory_space=pl.ANY)] * len(arrays),
        scratch_shapes=[
            pltpu.SemaphoreType.DMA((len(arrays),)),
            pltpu.SemaphoreType.DMA((copies,)),
            pltpu.SemaphoreType.DMA((copies,)),
        ],
        compiler_params=pltpu.CompilerParams(collective_id=0, has_side_effects=True),
        name="gather_weights",
    )(*shaped)


def scatter_kernel(grid, chunks, count, *refs):
    ins, outs = refs[:count], refs[count : 2 * count]
    rest = refs[2 * count :]
    held = rest[: len(chunks)]
    landed = rest[len(chunks) : 5 * len(chunks)]
    local_sem, send_sem, recv_sem = rest[5 * len(chunks) :]
    at = grid.here()
    grid.barrier(at)
    number = 0
    flying, locals_ = {}, []
    for ci, s in schedule(len(chunks), 5, 3):
        array, low, width, order = chunks[ci]
        columns = pl.ds(low, width)
        if s > 0:
            if s == 1:
                locals_[ci].wait()
            for copy in flying[ci, s - 1]:
                copy.wait_recv()
            done = order[:s]
            arrived = landed[4 * ci + s - 1]
            sizes = [1 if a in done else grid.size[a] for a in "xczy"]
            fixed = [
                0 if a == "c" else (at[a] if a in done else None) for a in "xczy"
            ]
            total = sizes[0] * sizes[1] * sizes[2] * sizes[3]
            peers = grid.size[order[s - 1]] - 1

            def add(i, carry, s=s, ci=ci, array=array, columns=columns, sizes=sizes, fixed=fixed,
                    arrived=arrived, peers=peers):
                place, spot, left = [], [], i
                for n, at_fixed in reversed(list(zip(sizes, fixed))):
                    part = 0 if n == 1 else lax.rem(left, n)
                    left = left if n == 1 else lax.div(left, n)
                    spot.append(part)
                    place.append(part if at_fixed is None else at_fixed)
                place, spot = tuple(reversed(place)), tuple(reversed(spot))
                value = held[ci][place].astype(jnp.float32)
                for k in range(peers):
                    value = value + arrived[(k,) + spot].astype(jnp.float32)
                if s == 4:
                    outs[array][:, columns] = value
                else:
                    held[ci][place] = value.astype(held[ci].dtype)
                return carry

            if total == 1:
                add(0, 0)
            else:
                lax.fori_loop(0, total, add, 0)
        if s == 4:
            continue
        axis = order[s]
        done = order[:s]
        if s == 0:
            index = tuple(pl.ds(at[a], 1) if a == "c" else slice(None) for a in "xczy")
            copy = pltpu.make_async_copy(
                ins[array].at[index + (slice(None), columns)], held[ci], local_sem.at[ci]
            )
            copy.start()
            locals_.append(copy)
        flying[ci, s] = []
        for k in range(1, grid.size[axis]):
            target = grid.step(at, axis, k)
            index = []
            for a in "xczy":
                if a == axis:
                    index.append(pl.ds(target[a], 1))
                elif a in done and a != "c":
                    index.append(pl.ds(at[a], 1))
                else:
                    index.append(slice(None))
            index = tuple(index)
            if s == 0:
                source = ins[array].at[index + (slice(None), columns)]
            else:
                source = held[ci].at[index]
            copy = pltpu.make_async_remote_copy(
                src_ref=source,
                dst_ref=landed[4 * ci + s].at[k - 1],
                send_sem=send_sem.at[number],
                recv_sem=recv_sem.at[number],
                device_id=grid.device(target),
                device_id_type=MESH,
            )
            copy.start()
            number += 1
            flying[ci, s].append(copy)
    for copies in flying.values():
        for copy in copies:
            copy.wait_send()


def scatter_sums(grid, arrays, chunks):
    per_chunk = sum(n - 1 for n in grid.size.values())
    copies = per_chunk * len(chunks)
    held, landed = [], []
    for array, _, width, order in chunks:
        dtype, rows = arrays[array].dtype, arrays[array].shape[-2]
        shape = [1 if a == "c" else grid.size[a] for a in "xczy"] + [rows, width]
        held.append(pltpu.VMEM(tuple(shape), dtype))
        for s in range(4):
            part = [1 if a in order[: s + 1] else grid.size[a] for a in "xczy"] + [rows, width]
            landed.append(pltpu.VMEM((max(grid.size[order[s]] - 1, 1),) + tuple(part), dtype))
    return pl.pallas_call(
        functools.partial(scatter_kernel, grid, chunks, len(arrays)),
        out_shape=[jax.ShapeDtypeStruct(a.shape[-2:], jnp.float32) for a in arrays],
        in_specs=[pl.BlockSpec(memory_space=pl.ANY)] * len(arrays),
        out_specs=[pl.BlockSpec(memory_space=pltpu.VMEM)] * len(arrays),
        scratch_shapes=held
        + landed
        + [
            pltpu.SemaphoreType.DMA((len(chunks),)),
            pltpu.SemaphoreType.DMA((copies,)),
            pltpu.SemaphoreType.DMA((copies,)),
        ],
        compiler_params=pltpu.CompilerParams(
            collective_id=1, has_side_effects=True, vmem_limit_bytes=48 * 1024 * 1024
        ),
        name="scatter_grads",
    )(*arrays)


def swap_halves(values, first_half, half_dim):
    lanes = values.shape[-1]
    down = pltpu.roll(values, lanes - half_dim, 1)
    up = pltpu.roll(values, half_dim, 1)
    return jnp.where(first_half, down, up)


def lane_masks(rows):
    lane = lax.broadcasted_iota(jnp.int32, (rows, LANES), 1)
    return lane, lax.rem(lane, HEAD_DIM) < HEAD_DIM // 2


def forward_kernel(scale, q_ref, k_ref, v_ref, cos_ref, sin_ref, col_ref, row_ref,
                   rq_ref, rk_ref, rv_ref, att_ref, prob_ref):
    rows = q_ref.shape[0]
    lane, first_half = lane_masks(rows)
    cosine, sine = cos_ref[...], sin_ref[...]
    q, k = q_ref[...], k_ref[...]
    half = HEAD_DIM // 2
    rq = (q * cosine + swap_halves(q, first_half, half) * sine).astype(jnp.bfloat16)
    rk = (k * cosine + swap_halves(k, first_half, half) * sine).astype(jnp.bfloat16)
    rv = v_ref[...].astype(jnp.bfloat16)
    rq_ref[...], rk_ref[...], rv_ref[...] = rq, rk, rv
    i = lax.broadcasted_iota(jnp.int32, (rows, rows), 0)
    j = lax.broadcasted_iota(jnp.int32, (rows, rows), 1)
    allowed = (col_ref[...] == row_ref[...]) & (jnp.abs(i - j) <= HALF_WINDOW)
    result = jnp.zeros((rows, LANES), jnp.float32)
    for h in range(LANES // HEAD_DIM):
        mine = lax.div(lane, HEAD_DIM) == h
        scores = times_transposed(jnp.where(mine, rq, jnp.zeros_like(rq)), rk) * scale
        scores = jnp.where(allowed, scores, big_negative)
        top = jnp.max(scores, axis=-1, keepdims=True)
        weights = jnp.exp(scores - top)
        prob = weights * (1.0 / jnp.sum(weights, axis=-1, keepdims=True))
        prob_ref[h] = prob
        part = jnp.dot(prob.astype(jnp.bfloat16), rv, preferred_element_type=jnp.float32)
        result = jnp.where(mine, part, result)
    att_ref[...] = result.astype(jnp.bfloat16)


def backward_kernel(scale, rq_ref, rk_ref, rv_ref, att_ref, datt_ref, prob_ref, cos_ref, sin_ref,
                    out_ref):
    rows = rq_ref.shape[0]
    width = out_ref.shape[1] // 3
    lane, first_half = lane_masks(rows)
    rq, rk, rv, datt = rq_ref[...], rk_ref[...], rv_ref[...], datt_ref[...]
    product = datt.astype(jnp.float32) * att_ref[...].astype(jnp.float32)
    dq = jnp.zeros((rows, LANES), jnp.float32)
    dk, dv = dq, dq
    for h in range(LANES // HEAD_DIM):
        mine = lax.div(lane, HEAD_DIM) == h
        delta = jnp.sum(jnp.where(mine, product, 0.0), axis=-1, keepdims=True)
        dprob = times_transposed(jnp.where(mine, datt, jnp.zeros_like(datt)), rv)
        prob = prob_ref[h]
        dscores = (prob * (dprob - delta) * scale).astype(jnp.bfloat16)
        dv = jnp.where(mine, contract_rows(prob.astype(jnp.bfloat16), datt), dv)
        dq = jnp.where(mine, jnp.dot(dscores, rk, preferred_element_type=jnp.float32), dq)
        dk = jnp.where(mine, contract_rows(dscores, rq), dk)
    cosine, sine = cos_ref[...], sin_ref[...]
    half = HEAD_DIM // 2
    dq = dq * cosine - swap_halves(dq, first_half, half) * sine
    dk = dk * cosine - swap_halves(dk, first_half, half) * sine
    at = pl.program_id(0) * LANES
    for part, value in enumerate((dq, dk, dv)):
        columns = pl.ds(pl.multiple_of(part * width + at, LANES), LANES)
        out_ref[:, columns] = value.astype(jnp.bfloat16)


def attention_forward(projected, cosine, sine, starts, scale):
    rows, width = projected.shape[0], projected.shape[1] // 3
    pairs = width // LANES
    heads = LANES // HEAD_DIM
    block = lambda offset: pl.BlockSpec((rows, LANES), lambda j: (0, j + offset))
    whole = lambda shape: pl.BlockSpec(shape, lambda j: (0, 0))
    wide = jax.ShapeDtypeStruct((rows, width), jnp.bfloat16)
    return pl.pallas_call(
        functools.partial(forward_kernel, scale),
        grid=(pairs,),
        in_specs=[block(0), block(pairs), block(2 * pairs), whole((rows, LANES)),
                  whole((rows, LANES)), whole((rows, 1)), whole((1, rows))],
        out_specs=[block(0)] * 4 + [pl.BlockSpec((heads, rows, rows), lambda j: (j, 0, 0))],
        out_shape=[wide] * 4 + [jax.ShapeDtypeStruct((pairs * heads, rows, rows), jnp.float32)],
        name="attention_forward",
    )(projected, projected, projected, cosine, sine, starts[:, None], starts[None, :])


def attention_backward(rq, rk, rv, attended, d_attended, prob, cosine, sine, scale):
    rows, width = rq.shape
    pairs = width // LANES
    heads = LANES // HEAD_DIM
    block = pl.BlockSpec((rows, LANES), lambda j: (0, j))
    whole = lambda shape: pl.BlockSpec(shape, lambda j: (0, 0))
    return pl.pallas_call(
        functools.partial(backward_kernel, scale),
        grid=(pairs,),
        in_specs=[block] * 5 + [pl.BlockSpec((heads, rows, rows), lambda j: (j, 0, 0)),
                  whole((rows, LANES)), whole((rows, LANES))],
        out_specs=whole((rows, 3 * width)),
        out_shape=jax.ShapeDtypeStruct((rows, 3 * width), jnp.bfloat16),
        name="attention_backward",
    )(rq, rk, rv, attended, d_attended, prob, cosine, sine)


PIECE = 384
GATHER_CYCLE = ('zyxc', 'zxyc', 'zyxc', 'zxyc', 'yzxc', 'xzyc')
SCATTER_CYCLE = ('cxyz', 'cyxz')


def pieces(array, columns, orders):
    piece = PIECE if columns % PIECE == 0 else columns
    return [
        (array, low, piece, tuple(orders[n % len(orders)]))
        for n, low in enumerate(range(0, columns, piece))
    ]


def body(
    grid,
    tokens,
    cotangent,
    starts,
    attention_norm_scale,
    w_qkv,
    w_out,
    feedforward_norm_scale,
    w_in,
    w_down,
):
    row_count, width = tokens.shape
    units = w_down.shape[0]
    scale = HEAD_DIM ** (-0.5)
    owned = w_qkv.shape[0]
    devices = width // owned
    axes = ("dp", "fsdp")
    kernels = owned % 8 == 0 and owned <= LANES
    out_t, down_t = w_out.T, w_down.T
    if kernels:
        scales = jnp.pad(
            jnp.stack([attention_norm_scale, feedforward_norm_scale]),
            ((0, 14), (0, LANES - owned)),
        )
        parts = [scales, w_qkv, out_t, w_in, down_t]
        chunks = [(0, 0, LANES, tuple(GATHER_CYCLE[0]))]
        chunks += pieces(1, w_qkv.shape[1], GATHER_CYCLE)
        chunks += pieces(2, width, GATHER_CYCLE)
        chunks += pieces(3, w_in.shape[1], GATHER_CYCLE)
        chunks += pieces(4, units, GATHER_CYCLE)
        all_scales, full_qkv, full_out_t, full_in, full_down_t = gather_all(grid, parts, chunks)
        all_scales = all_scales.reshape(devices, 16, LANES)
        attention_scale = all_scales[:, 0, :owned].reshape(width)
        feedforward_scale = all_scales[:, 1, :owned].reshape(width)
        full_qkv, full_out_t, full_in, full_down_t = (
            a.reshape(width, a.shape[-1]) for a in (full_qkv, full_out_t, full_in, full_down_t)
        )
    else:
        full_qkv, full_out_t, full_in, full_down_t, attention_scale, feedforward_scale = (
            lax.all_gather(a, axes, axis=0, tiled=True)
            for a in (w_qkv, out_t, w_in, down_t, attention_norm_scale, feedforward_norm_scale)
        )
    attention_scale = attention_scale.astype(jnp.float32)
    feedforward_scale = feedforward_scale.astype(jnp.float32)
    slot = jnp.arange(row_count, dtype=jnp.int32)
    valid = starts < row_count
    position = slot - starts
    input_float = tokens.astype(jnp.float32)
    first_standardized, first_inverse_deviation = apply_layer_norm(input_float)
    first_normalized = (first_standardized * attention_scale).astype(jnp.bfloat16)
    projected = jnp.dot(first_normalized, full_qkv, preferred_element_type=jnp.float32)
    cosine, sine = rotary_tables(position, HEAD_DIM)
    repeats = LANES // HEAD_DIM
    cosine = jnp.tile(jnp.concatenate([cosine, cosine], 1), (1, repeats))
    sine = jnp.tile(jnp.concatenate([-sine, sine], 1), (1, repeats))
    rq, rk, rv, attended, prob = attention_forward(projected, cosine, sine, starts, scale)
    hidden_state = input_float + times_transposed(attended, full_out_t)
    second_standardized, second_inverse_deviation = apply_layer_norm(hidden_state)
    second_normalized = (second_standardized * feedforward_scale).astype(jnp.bfloat16)
    gate_up = jnp.dot(second_normalized, full_in, preferred_element_type=jnp.float32)
    pre_act = gate_up[:, :units]
    gate_half = gate_up[:, units:]
    activated, slope = gelu_parts(pre_act)
    hidden = (activated * gate_half).astype(jnp.bfloat16)
    output = (hidden_state + times_transposed(hidden, full_down_t)).astype(jnp.bfloat16)
    grad_out = jnp.where(valid[:, None], cotangent, jnp.zeros_like(cotangent))
    down_grad_t = contract_rows(grad_out, hidden)
    d_hidden = jnp.dot(grad_out, full_down_t, preferred_element_type=jnp.float32)
    d_gu = jnp.concatenate([d_hidden * gate_half * slope, d_hidden * activated], 1).astype(
        jnp.bfloat16
    )
    second_normalized_gradient = times_transposed(d_gu, full_in)
    mixed_gradient, feedforward_scale_gradient = norm_backward(
        second_normalized_gradient,
        second_standardized,
        second_inverse_deviation,
        feedforward_scale,
    )
    d_state = grad_out.astype(jnp.float32) + mixed_gradient
    d_state_b = d_state.astype(jnp.bfloat16)
    out_grad_t = contract_rows(d_state_b, attended)
    d_attended = jnp.dot(d_state_b, full_out_t, preferred_element_type=jnp.float32).astype(
        jnp.bfloat16
    )
    d_qkv = attention_backward(rq, rk, rv, attended, d_attended, prob, cosine, sine, scale)
    first_normalized_gradient = times_transposed(d_qkv, full_qkv)
    norm_input_gradient, attention_scale_gradient = norm_backward(
        first_normalized_gradient,
        first_standardized,
        first_inverse_deviation,
        attention_scale,
    )
    input_grad = d_state + norm_input_gradient
    qkv_whole = contract_rows(first_normalized, d_qkv)
    in_whole = contract_rows(second_normalized, d_gu)
    every_grad = (in_whole, down_grad_t, out_grad_t, qkv_whole)
    gains = (attention_scale_gradient, feedforward_scale_gradient)
    if kernels:
        gains = jnp.stack(gains).reshape(2, devices, owned).transpose(1, 0, 2)
        gains = jnp.pad(gains, ((0, 0), (0, 6), (0, LANES - owned)))
        parts = [a.astype(jnp.bfloat16).reshape(grid.shape() + (owned, a.shape[-1])) for a in every_grad]
        parts.append(gains.reshape(grid.shape() + (8, LANES)))
        chunks = pieces(0, in_whole.shape[1], SCATTER_CYCLE)
        chunks += pieces(1, units, SCATTER_CYCLE)
        chunks += pieces(2, width, SCATTER_CYCLE)
        chunks += pieces(3, qkv_whole.shape[1], SCATTER_CYCLE)
        chunks += [(4, 0, LANES, tuple(SCATTER_CYCLE[0]))]
        in_owned, down_owned_t, out_owned_t, qkv_owned, gains = scatter_sums(grid, parts, chunks)
        gain_a_owned, gain_m_owned = gains[0, :owned], gains[1, :owned]
    else:
        in_owned, down_owned_t, out_owned_t, qkv_owned, gain_a_owned, gain_m_owned = (
            lax.psum_scatter(a, axes, scatter_dimension=0, tiled=True) for a in every_grad + gains
        )
    return (
        output,
        input_grad,
        qkv_owned,
        out_owned_t.T,
        in_owned,
        down_owned_t.T,
        gain_a_owned,
        gain_m_owned,
    )


def solution(mesh):
    return jax.shard_map(
        functools.partial(body, Grid(mesh.shape["dp"], mesh.shape["fsdp"])),
        mesh=mesh,
        in_specs=(
            P(("dp", "fsdp"), None),
            P(("dp", "fsdp"), None),
            P(("dp", "fsdp")),
            P(("dp", "fsdp")),
            P(("dp", "fsdp"), None),
            P(None, ("dp", "fsdp")),
            P(("dp", "fsdp")),
            P(("dp", "fsdp"), None),
            P(None, ("dp", "fsdp")),
        ),
        out_specs=(
            P(("dp", "fsdp"), None),
            P(("dp", "fsdp"), None),
            P(("dp", "fsdp"), None),
            P(None, ("dp", "fsdp")),
            P(("dp", "fsdp"), None),
            P(None, ("dp", "fsdp")),
            P(("dp", "fsdp")),
            P(("dp", "fsdp")),
        ),
        check_vma=False,
    )
```
